32 devices in a mesh: dom: 2 (over y), wide: 16 (over z, x, core).
Axes of the slice: x: 2, y: 2, z: 4, core: 2. Of those that a mesh axis runs over, the one named last changes fastest.
Arguments:
- embeddings: bfloat16 [16384, 768], P(('dom', 'wide')), parts along dimension 0, may hold values from -6 to 6
- cluster_id: int32 [16384, 1], P(('dom', 'wide')), parts along dimension 0, may hold values from 0 to 7; in each aligned block of 512 rows (0 to 511, 512 to 1023, ...) at most 160 rows name the same one
Outputs:
- max_similarity: float32 [16384], P(('dom', 'wide')), parts along dimension 0
The draws below stay inside these ranges and needn't reach their ends.
There are 2 independent parts, one for each index of `dom`. The reference program is written for one: setup_inputs(seed, part) draws one part's arguments, and reference() takes and returns one part's arrays. A program takes and returns all parts, laid end to end along the dimension named above; each array names one. Nothing has to cross between parts.
Inputs may be any that keep to these rules, and one draw needn't show every extreme that they name: `cluster_id`: among the 512 rows of one device (aligned blocks of 512 rows), no cluster appears more than 160 times; every cluster has some row.
All inputs are finite; a program needn't handle non-finite values.
Results may differ from the reference program's by a relative error of at most 0.0014.
Values may be sent and summed in bfloat16 or wider, within the bound.
A program may use at most 64 MiB of HBM per device.

```python
import math
import jax
import jax.numpy as jnp
import numpy as np
from jax import lax

D = 768
ROW_DEV = 512
CLUSTERS = 8
MOST = 160
ROWS = 8192
N_WIDE = 16


def steps_of(own_key, shape, pieces, smallest, high):
    factor_of, own = 1.0, jax.random.fold_in(own_key, 6)
    for axis_at, parts in pieces:
        steps = jnp.exp(jax.random.uniform(jax.random.fold_in(own, axis_at), (parts,), jnp.float32, smallest / len(pieces), high / len(pieces)))
        factor_of = factor_of * jnp.repeat(steps, shape[axis_at] // parts).reshape([-1 if axis == axis_at else 1 for axis in range(len(shape))])
    return factor_of


def deal_out(stream_key, own, number, rows, count, top, bound, lean):
    ranking = jax.random.permutation(stream_key, count)
    packed, common = portions_of(count, rows * top, bound, lean, True), portions_of(count, rows * top, bound, lean, False)
    places = jnp.arange(count)

    def named(lengths, offset_by):
        used = int((lengths > 0).sum())
        fixed = max(1, used // 4)
        shifted = fixed + (places - fixed + offset_by * (used - fixed)) % max(1, count - fixed)
        return jnp.zeros((count,), jnp.int32).at[ranking[jnp.where(places < fixed, places, shifted)]].set(jnp.asarray(lengths, jnp.int32))

    lengths = jnp.where(number % 4 == 0, named(packed, number // 4), named(common, number - number // 4 - 1))
    mixed = jax.random.permutation(jax.random.fold_in(own, 3), count)
    donor, taker = mixed[0:count // 2 * 2:2], mixed[1:count // 2 * 2:2]
    margin = jnp.minimum(lengths[donor] - 1, bound - lengths[taker]) // 2
    margin = jnp.where((donor == ranking[0]) | (taker == ranking[0]) | (lengths[taker] == 0), 0, jnp.maximum(margin, 0))
    shifted = jax.random.randint(jax.random.fold_in(own, 4), (count // 2,), 0, 1 << 20) % (margin + 1)
    lengths = lengths.at[donor].add(-shifted).at[taker].add(shifted)
    members = jnp.searchsorted(jnp.cumsum(lengths), jnp.arange(rows * top), side="right").astype(jnp.int32)
    listing = members.reshape(top, rows).T
    listing = listing[jax.random.permutation(jax.random.fold_in(own, 1), rows)]
    offset_by = jax.random.randint(jax.random.fold_in(own, 2), (rows, 1), 0, top)
    return jnp.take_along_axis(listing, (jnp.arange(top)[None, :] + offset_by) % top, axis=1)


def portions_of(amount, total, reach, lean, full):
    portions = [(1 << 20) // math.isqrt(standing ** lean) + 1 for standing in range(1, amount + 1)]
    largest = reach if full else min(reach, max(-(-total // amount), total * portions[0] // sum(portions)))
    least = 1 if total - largest >= amount - 1 else 0
    holding, rest = [largest] + [least] * (amount - 1), total - largest - least * (amount - 1)
    while rest > 0:
        candidates = [i for i in range(1, amount) if holding[i] < largest] or [i for i in range(1, amount) if holding[i] < reach]
        whole, remaining = sum([portions[i] for i in candidates]), rest
        for i in candidates:
            extra = min(reach - holding[i], max(1, remaining * portions[i] // whole), rest)
            holding[i] = holding[i] + extra
            rest = rest - extra
    return np.array(holding)


def noise(own_key, extent, width, reach, cuts=(), kind=jnp.bfloat16):
    gain = steps_of(own_key, extent, cuts, -0.22, 0.18) if cuts else 1.0
    entries = jax.random.normal(own_key, extent, jnp.float32) * width * gain
    return jnp.minimum(jnp.maximum(entries, -reach), reach).astype(kind)


def setup_inputs(seed: int = 0, part: int = 0) -> dict:
    key_of = jax.random.split(jax.random.key(seed), 3)
    part_splits = jax.random.split(jax.random.fold_in(key_of[2], part), 3)
    embeddings = noise(part_splits[0], (ROWS, D), 1.0, 6.0, ((0, 16),))
    cluster_id_keys = jax.random.split(jax.random.fold_in(part_splits[1], 1), ROWS // ROW_DEV)
    cluster_id_turns = jax.random.permutation(jax.random.fold_in(part_splits[1], 3), ROWS // ROW_DEV)
    cluster_id = jax.vmap(lambda own, number: deal_out(jax.random.fold_in(part_splits[1], 2), own, number, ROW_DEV, CLUSTERS, 1, MOST, 1))(cluster_id_keys, cluster_id_turns).reshape((ROWS, 1))
    return {"embeddings": embeddings, "cluster_id": cluster_id}


def normalize(embedded):
    values = embedded.astype(jnp.float32)
    inverse = lax.rsqrt(lax.optimization_barrier(jnp.mean(values * values, axis=1, keepdims=True)) + 1e-06)
    return (values * inverse * (1.0 / math.sqrt(values.shape[1]))).astype(jnp.bfloat16)

def reference(embeddings, cluster_id):
    unit_rows = normalize(embeddings).astype(jnp.float32)
    labels = cluster_id[:, 0].astype(jnp.int32)
    sorted_index = jnp.argsort(labels, stable=True).astype(jnp.int32)
    sorted_rows = unit_rows[sorted_index]
    sorted_labels = labels[sorted_index]
    window = MOST * N_WIDE
    feature_dim = unit_rows.shape[1]
    padded_rows = jnp.concatenate([jnp.zeros((window, feature_dim), jnp.float32), sorted_rows], axis=0)
    padded_labels = jnp.concatenate([jnp.full((window,), -1, jnp.int32), sorted_labels], axis=0)
    positions = jnp.arange(ROWS, dtype=jnp.int32)
    padded_positions = jnp.concatenate([jnp.full((window,), -1, jnp.int32), positions], axis=0)

    def block_max(start):
        queries = lax.dynamic_slice_in_dim(sorted_rows, start, ROW_DEV, 0)
        query_labels = lax.dynamic_slice_in_dim(sorted_labels, start, ROW_DEV, 0)
        query_positions = start + jnp.arange(ROW_DEV, dtype=jnp.int32)
        key_rows = lax.dynamic_slice_in_dim(padded_rows, start, window + ROW_DEV, 0)
        key_labels = lax.dynamic_slice_in_dim(padded_labels, start, window + ROW_DEV, 0)
        key_positions = lax.dynamic_slice_in_dim(padded_positions, start, window + ROW_DEV, 0)
        scores = jnp.dot(queries, key_rows.T, precision=lax.Precision.HIGHEST)
        allowed = (key_labels[None, :] == query_labels[:, None]) & (key_positions[None, :] < query_positions[:, None])
        return lax.optimization_barrier(jnp.max(jnp.where(allowed, scores, -1.0), axis=1))
    starts = jnp.arange(N_WIDE, dtype=jnp.int32) * ROW_DEV
    sorted_best = lax.map(block_max, starts).reshape(-1)
    return jnp.zeros((ROWS,), jnp.float32).at[sorted_index].set(sorted_best)
```

```python
import functools
import math

import jax
import jax.numpy as jnp
from jax import lax
from jax.experimental import pallas as pl
from jax.experimental.pallas import tpu as pltpu
from jax.sharding import PartitionSpec as P


def swapped(value, axis, bit):
    mask = 2**bit
    pairs = [(source, source ^ mask) for source in range(lax.axis_size(axis))]
    return lax.ppermute(value, axis, pairs)


def normalize(embedded):
    values = embedded.astype(jnp.float32)
    inverse = lax.rsqrt(jnp.mean(values * values, axis=1, keepdims=True) + 1e-06)
    return (values * inverse * (1.0 / math.sqrt(values.shape[1]))).astype(jnp.bfloat16)


def pair_scores(queries, key_rows):
    return jnp.einsum("qd,kd->qk", queries, key_rows, preferred_element_type=jnp.float32)


def masked_max(scores, allowed):
    return jnp.max(jnp.where(allowed, scores, -1.0), axis=1)


def per_device(embeddings, cluster_id):
    axis_size = lax.axis_size("wide")
    rows_dev = embeddings.shape[0]
    feature_dim = embeddings.shape[1]
    clusters = axis_size // 2
    capacity = (5 * rows_dev + 2 * axis_size - 1) // (2 * axis_size)
    buffer_rows = axis_size * capacity
    unit_rows = normalize(embeddings)
    labels = cluster_id[:, 0]
    my_index = lax.axis_index("wide")
    my_flip = my_index % 2
    position = lax.iota(jnp.int32, rows_dev)
    same_cluster = labels[:, None] == labels[None, :]
    earlier = position[None, :] < position[:, None]
    local_rank = jnp.sum((same_cluster & earlier).astype(jnp.int32), axis=1)
    target = 2 * labels + (local_rank + my_flip) % 2
    slot_index = target * capacity + local_rank // 2
    outgoing = jnp.zeros((buffer_rows, feature_dim), jnp.bfloat16).at[slot_index].set(unit_rows)
    cluster_count = jnp.sum(
        (labels[:, None] == lax.iota(jnp.int32, clusters)[None, :]).astype(jnp.int32), axis=0
    )
    parity = lax.iota(jnp.int32, axis_size) % 2
    send_count = (jnp.repeat(cluster_count, 2) + 1 - (parity + my_flip) % 2) // 2
    outgoing_blocks = outgoing.reshape(axis_size, capacity, feature_dim)
    count_blocks = send_count.reshape(axis_size, 1)
    received, counts = (
        lax.all_to_all(outgoing_blocks, "wide", split_axis=0, concat_axis=0, tiled=True),
        lax.all_to_all(count_blocks, "wide", split_axis=0, concat_axis=0, tiled=True),
    )
    own_rows = received.reshape(buffer_rows, feature_dim)
    partner, partner_counts = swapped((own_rows, counts), "wide", 0)
    side_bit = my_index % 2
    slot_pos = lax.iota(jnp.int32, capacity)
    sources = lax.iota(jnp.int32, axis_size)
    base_key = (sources[:, None] * (2 * capacity) + 2 * slot_pos[None, :]).reshape(-1)
    source_parity = jnp.repeat(sources % 2, capacity)
    own_key = base_key + (side_bit + source_parity) % 2
    partner_key = base_key + (1 - side_bit + source_parity) % 2
    own_live = (slot_pos[None, :] < counts).reshape(-1)
    partner_live = (slot_pos[None, :] < partner_counts).reshape(-1)
    blocks = 8
    query_rows = own_rows.reshape(blocks, -1, feature_dim)
    query_key = own_key.reshape(blocks, -1)

    def self_max(pieces):
        queries, keys_here = pieces
        return masked_max(
            pair_scores(queries, own_rows),
            own_live[None, :] & (own_key[None, :] < keys_here[:, None]),
        )

    self_best = lax.map(self_max, (query_rows, query_key)).reshape(-1)
    first = side_bit == 0
    left_rows = jnp.where(first, own_rows, partner)
    left_key = jnp.where(first, own_key, partner_key)
    left_live = jnp.where(first, own_live, partner_live)
    right_rows = jnp.where(first, partner, own_rows)
    right_key = jnp.where(first, partner_key, own_key)
    right_live = jnp.where(first, partner_live, own_live)
    half_rows = buffer_rows // 2
    start = side_bit * half_rows
    lower_rows = lax.dynamic_slice_in_dim(left_rows, start, half_rows, 0).reshape(
        blocks // 2, -1, feature_dim
    )
    lower_key = lax.dynamic_slice_in_dim(left_key, start, half_rows, 0).reshape(blocks // 2, -1)
    lower_live = lax.dynamic_slice_in_dim(left_live, start, half_rows, 0).reshape(blocks // 2, -1)

    def cross_max(pieces):
        queries, keys_here, live_here = pieces
        scores = pair_scores(queries, right_rows)
        row_best = masked_max(
            scores, right_live[None, :] & (right_key[None, :] < keys_here[:, None])
        )
        column_mask = live_here[:, None] & (keys_here[:, None] < right_key[None, :])
        column_best = jnp.max(jnp.where(column_mask, scores, -1.0), axis=0)
        return (row_best, column_best)

    row_best, column_best = lax.map(cross_max, (lower_rows, lower_key, lower_live))
    row_best = row_best.reshape(-1)
    column_best = jnp.max(column_best, axis=0)
    placed = lax.dynamic_update_slice_in_dim(
        jnp.full((buffer_rows,), -1.0, jnp.float32), row_best, start, 0
    )
    kept = jnp.where(first, placed, column_best)
    handed = jnp.where(first, column_best, placed)
    returned = swapped(handed, "wide", 0)
    best_all = jnp.maximum(self_best, jnp.maximum(kept, returned))
    back = lax.all_to_all(
        best_all.reshape(axis_size, capacity), "wide", split_axis=0, concat_axis=0, tiled=True
    )
    return back.reshape(-1)[slot_index]


LANES = 4
CHUNK = 128
MESH = pl.DeviceIdType.MESH


def grid_kernel(levels, x_ref, id_ref, out_ref, lev, lev_id, unit, left, left_id, right, right_id,
                acc, part, res, back, back_in, lev_send, lev_recv, left_send, left_recv,
                right_send, right_recv, res_send, res_recv, back_send, back_recv):
    me = lax.axis_index("wide")
    lane = lax.rem(me, LANES)
    level = me // LANES
    base = level * LANES
    half = levels // 2
    rows, width = x_ref.shape
    chunks = rows // CHUNK

    def peer(slot):
        low = lax.rem(lane, 2)
        high = lane // 2
        low = 1 - low if slot % 2 else low
        high = 1 - high if slot // 2 else high
        return base + 2 * high + low

    right_dev = me + LANES
    left_dev = me - LANES
    has_right = level < levels - 1
    sends_own = level < half
    takes_back = level == half
    gives_back = level == half + 1

    barrier = pltpu.get_barrier_semaphore()
    for slot in range(1, LANES):
        pl.semaphore_signal(barrier, inc=1, device_id={"wide": peer(slot)}, device_id_type=MESH)

    @pl.when(has_right)
    def _():
        pl.semaphore_signal(barrier, inc=1, device_id={"wide": right_dev}, device_id_type=MESH)

    @pl.when(level > 0)
    def _():
        pl.semaphore_signal(barrier, inc=1, device_id={"wide": left_dev}, device_id_type=MESH)

    peers = LANES - 1 + has_right.astype(jnp.int32) + (level > 0).astype(jnp.int32)
    pl.semaphore_wait(barrier, peers)

    def piece(block, ids, k):
        return ids if k == chunks else block.at[pl.ds(k * CHUNK, CHUNK)]

    order = [chunks] + list(range(chunks))

    def send(src, src_id, dst, dst_id, k, ssem, rsem, dev):
        return pltpu.make_async_remote_copy(
            src_ref=piece(src, src_id, k), dst_ref=piece(dst, dst_id, k),
            send_sem=ssem.at[k], recv_sem=rsem.at[k],
            device_id={"wide": dev}, device_id_type=MESH)

    def level_own(slot, k):
        return send(x_ref, id_ref, lev.at[slot - 1], lev_id.at[slot - 1], k,
                    lev_send.at[slot - 1], lev_recv.at[slot - 1], peer(slot))

    def level_pass(k):
        return send(lev.at[1], lev_id.at[1], lev.at[2], lev_id.at[2], k,
                    lev_send.at[2], lev_recv.at[2], peer(1))

    def right_own(k):
        return send(x_ref, id_ref, left.at[0], left_id.at[0], k,
                    left_send.at[0], left_recv.at[0], right_dev)

    def right_pass(j, to, k):
        return send(left.at[j], left_id.at[j], left.at[to], left_id.at[to], k,
                    left_send.at[to], left_recv.at[to], right_dev)

    def left_own(k):
        return send(x_ref, id_ref, right, right_id, k, right_send, right_recv, left_dev)

    for k in order:
        @pl.when(sends_own & has_right)
        def _(k=k):
            right_own(k).start()

        level_own(2, k).start()
        level_own(1, k).start()

        @pl.when(gives_back)
        def _(k=k):
            left_own(k).start()

    def normal(block):
        values = block.astype(jnp.float32)
        inverse = lax.rsqrt(jnp.mean(values * values, axis=1, keepdims=True) + 1e-06)
        return (values * inverse * (1.0 / math.sqrt(width))).astype(jnp.bfloat16)

    def column(ids, k):
        row = ids[:, k * CHUNK:(k + 1) * CHUNK]
        return jnp.transpose(jnp.broadcast_to(row, (CHUNK, CHUNK)))[:, :1]

    def scores(keys, queries):
        return lax.dot_general(keys, queries, (((1,), (1,)), ((), ())),
                               preferred_element_type=jnp.float32)

    def fold(values):
        count, wide_by = values.shape
        return jnp.max(values.reshape(count // 8, 8, wide_by), axis=0)

    def forward(j, k):
        if j + 1 < left.shape[0]:
            @pl.when(has_right & sends_own)
            def _():
                right_pass(j, j + 1, k).start()

        @pl.when(has_right & jnp.logical_not(sends_own))
        def _():
            right_pass(j, j, k).start()

    def ids_of(slot):
        return id_ref if slot == 0 else lev_id.at[slot - 1]

    def unit_chunk(slot, k):
        at = pl.ds(k * CHUNK, CHUNK)
        unit[slot, at, :] = normal(x_ref[at, :] if slot == 0 else lev[slot - 1, at, :])

    acc[...] = jnp.full_like(acc, -1.0)
    for k in range(chunks):
        unit_chunk(0, k)

    def own_level(slot):
        ids = ids_of(slot)
        best = acc[0]
        for k in range(chunks):
            value = scores(unit[slot, pl.ds(k * CHUNK, CHUNK), :], unit[0])
            keep = column(ids[...], k) == id_ref[...]
            if slot == 0:
                key_at = lax.broadcasted_iota(jnp.int32, value.shape, 0) + k * CHUNK
                keep = keep & (key_at < lax.broadcasted_iota(jnp.int32, value.shape, 1))
            best = jnp.maximum(best, fold(jnp.where(keep, value, -1.0)))
        acc[0] = best

    own_level(0)
    for k in order:
        @pl.when(level > 0)
        def _(k=k):
            right_own(k).wait_recv()
            forward(0, k)

        level_own(2, k).wait_recv()
        level_pass(k).start()
        level_own(1, k).wait_recv()
        if k < chunks:
            unit_chunk(1, k)
            unit_chunk(2, k)
    for k in order:
        level_pass(k).wait_recv()
        if k < chunks:
            unit_chunk(3, k)

    for slot in range(1, LANES):
        @pl.when(peer(slot) < me)
        def _(slot=slot):
            own_level(slot)

    def from_left(j, k):
        keys = normal(left[j, pl.ds(k * CHUNK, CHUNK), :])
        ids = column(left_id[j], k)
        for slot in range(LANES):
            value = scores(keys, unit[slot])
            value = jnp.where(ids == ids_of(slot)[...], value, -1.0)
            acc[slot] = jnp.maximum(acc[slot], fold(value))

    def from_right(k):
        at = pl.ds(k * CHUNK, CHUNK)
        queries = normal(right[at, :])
        ids = right_id[:, k * CHUNK:(k + 1) * CHUNK]
        best = jnp.full((8, CHUNK), -1.0, jnp.float32)
        for slot in range(LANES):
            for i in range(chunks):
                value = scores(unit[slot, pl.ds(i * CHUNK, CHUNK), :], queries)
                keep = column(ids_of(slot)[...], i) == ids
                best = jnp.maximum(best, fold(jnp.where(keep, value, -1.0)))
        back[:, k * CHUNK:(k + 1) * CHUNK] = jnp.max(best, axis=0, keepdims=True)

    def back_copy():
        return pltpu.make_async_remote_copy(
            src_ref=back, dst_ref=back_in, send_sem=back_send, recv_sem=back_recv,
            device_id={"wide": right_dev}, device_id_type=MESH)

    for j in range(1, half):
        for k in order:
            @pl.when(level > j)
            def _(j=j, k=k):
                right_pass(j - 1, j, k).wait_recv()
                forward(j, k)

            if k < chunks:
                @pl.when(level >= j)
                def _(j=j, k=k):
                    from_left(j - 1, k)

            if j == half - 1:
                @pl.when(takes_back & has_right)
                def _(k=k):
                    left_own(k).wait_recv()
                    if k < chunks:
                        from_right(k)

                if k == chunks - 1:
                    @pl.when(takes_back & has_right)
                    def _():
                        back_copy().start()

                if k < chunks:
                    @pl.when(level > j)
                    def _(j=j, k=k):
                        from_left(j, k)

    def res_copy(slot):
        return pltpu.make_async_remote_copy(
            src_ref=part.at[slot - 1], dst_ref=res.at[slot - 1], send_sem=res_send.at[slot - 1],
            recv_sem=res_recv.at[slot - 1], device_id={"wide": peer(slot)}, device_id_type=MESH)

    for slot in (3, 2, 1):
        part[slot - 1] = jnp.max(acc[slot], axis=0, keepdims=True)
        res_copy(slot).start()
    out_ref[...] = jnp.max(acc[0], axis=0, keepdims=True)

    @pl.when(gives_back)
    def _():
        back_copy().wait_recv()
        out_ref[...] = jnp.maximum(out_ref[...], back_in[...])

    for slot in range(1, LANES):
        res_copy(slot).wait_recv()
        out_ref[...] = jnp.maximum(out_ref[...], res[slot - 1])

    for slot in range(1, LANES):
        res_copy(slot).wait_send()
    for k in order:
        level_own(2, k).wait_send()
        level_own(1, k).wait_send()
        level_pass(k).wait_send()

        @pl.when(sends_own & has_right)
        def _(k=k):
            right_own(k).wait_send()

        @pl.when(gives_back)
        def _(k=k):
            left_own(k).wait_send()

        for j in range(half):
            if j + 1 < half:
                @pl.when(has_right & sends_own & (level > j))
                def _(j=j, k=k):
                    right_pass(j, j + 1, k).wait_send()

            @pl.when(has_right & jnp.logical_not(sends_own))
            def _(j=j, k=k):
                right_pass(j, j, k).wait_send()

    @pl.when(takes_back & has_right)
    def _():
        back_copy().wait_send()


def grid_plan(levels, embeddings, cluster_id):
    rows, width = embeddings.shape
    half = levels // 2
    pieces = rows // CHUNK + 1
    bf16, i32, f32 = jnp.bfloat16, jnp.int32, jnp.float32
    dma = pltpu.SemaphoreType.DMA
    best = pl.pallas_call(
        functools.partial(grid_kernel, levels),
        out_shape=jax.ShapeDtypeStruct((1, rows), f32),
        in_specs=[pl.BlockSpec(memory_space=pltpu.VMEM)] * 2,
        out_specs=pl.BlockSpec(memory_space=pltpu.VMEM),
        scratch_shapes=[
            pltpu.VMEM((LANES - 1, rows, width), bf16), pltpu.VMEM((LANES - 1, 1, rows), i32),
            pltpu.VMEM((LANES, rows, width), bf16),
            pltpu.VMEM((half, rows, width), bf16), pltpu.VMEM((half, 1, rows), i32),
            pltpu.VMEM((rows, width), bf16), pltpu.VMEM((1, rows), i32),
            pltpu.VMEM((LANES, 8, rows), f32),
            pltpu.VMEM((LANES - 1, 1, rows), f32), pltpu.VMEM((LANES - 1, 1, rows), f32),
            pltpu.VMEM((1, rows), f32), pltpu.VMEM((1, rows), f32),
            dma((LANES - 1, pieces)), dma((LANES - 1, pieces)),
            dma((half, pieces)), dma((half, pieces)),
            dma((pieces,)), dma((pieces,)),
            dma((LANES - 1,)), dma((LANES - 1,)), dma, dma,
        ],
        compiler_params=pltpu.CompilerParams(
            collective_id=0, has_side_effects=True, vmem_limit_bytes=40 * 2**20),
    )(embeddings, cluster_id.reshape(1, rows))
    return best.reshape(-1)


def solution(mesh):
    placed = (P(("dom", "wide"), None), P(("dom", "wide"), None))
    levels = mesh.shape["wide"] // LANES
    fits = levels == 4 and mesh.shape["wide"] % LANES == 0
    plan = functools.partial(grid_plan, levels) if fits else per_device
    return jax.shard_map(
        plan, mesh=mesh, in_specs=placed, out_specs=P(("dom", "wide")), check_vma=False
    )
```

```python
import functools
import math

import jax
import jax.numpy as jnp
from jax import lax
from jax.experimental import pallas as pl
from jax.experimental.pallas import tpu as pltpu
from jax.sharding import PartitionSpec as P


def swapped(value, axis, bit):
    mask = 2**bit
    pairs = [(source, source ^ mask) for source in range(lax.axis_size(axis))]
    return lax.ppermute(value, axis, pairs)


def normalize(embedded):
    values = embedded.astype(jnp.float32)
    inverse = lax.rsqrt(jnp.mean(values * values, axis=1, keepdims=True) + 1e-06)
    return (values * inverse * (1.0 / math.sqrt(values.shape[1]))).astype(jnp.bfloat16)


def pair_scores(queries, key_rows):
    return jnp.einsum("qd,kd->qk", queries, key_rows, preferred_element_type=jnp.float32)


def masked_max(scores, allowed):
    return jnp.max(jnp.where(allowed, scores, -1.0), axis=1)


def per_device(embeddings, cluster_id):
    axis_size = lax.axis_size("wide")
    rows_dev = embeddings.shape[0]
    feature_dim = embeddings.shape[1]
    clusters = axis_size // 2
    capacity = (5 * rows_dev + 2 * axis_size - 1) // (2 * axis_size)
    buffer_rows = axis_size * capacity
    unit_rows = normalize(embeddings)
    labels = cluster_id[:, 0]
    my_index = lax.axis_index("wide")
    my_flip = my_index % 2
    position = lax.iota(jnp.int32, rows_dev)
    same_cluster = labels[:, None] == labels[None, :]
    earlier = position[None, :] < position[:, None]
    local_rank = jnp.sum((same_cluster & earlier).astype(jnp.int32), axis=1)
    target = 2 * labels + (local_rank + my_flip) % 2
    slot_index = target * capacity + local_rank // 2
    outgoing = jnp.zeros((buffer_rows, feature_dim), jnp.bfloat16).at[slot_index].set(unit_rows)
    cluster_count = jnp.sum(
        (labels[:, None] == lax.iota(jnp.int32, clusters)[None, :]).astype(jnp.int32), axis=0
    )
    parity = lax.iota(jnp.int32, axis_size) % 2
    send_count = (jnp.repeat(cluster_count, 2) + 1 - (parity + my_flip) % 2) // 2
    outgoing_blocks = outgoing.reshape(axis_size, capacity, feature_dim)
    count_blocks = send_count.reshape(axis_size, 1)
    received, counts = (
        lax.all_to_all(outgoing_blocks, "wide", split_axis=0, concat_axis=0, tiled=True),
        lax.all_to_all(count_blocks, "wide", split_axis=0, concat_axis=0, tiled=True),
    )
    own_rows = received.reshape(buffer_rows, feature_dim)
    partner, partner_counts = swapped((own_rows, counts), "wide", 0)
    side_bit = my_index % 2
    slot_pos = lax.iota(jnp.int32, capacity)
    sources = lax.iota(jnp.int32, axis_size)
    base_key = (sources[:, None] * (2 * capacity) + 2 * slot_pos[None, :]).reshape(-1)
    source_parity = jnp.repeat(sources % 2, capacity)
    own_key = base_key + (side_bit + source_parity) % 2
    partner_key = base_key + (1 - side_bit + source_parity) % 2
    own_live = (slot_pos[None, :] < counts).reshape(-1)
    partner_live = (slot_pos[None, :] < partner_counts).reshape(-1)
    blocks = 8
    query_rows = own_rows.reshape(blocks, -1, feature_dim)
    query_key = own_key.reshape(blocks, -1)

    def self_max(pieces):
        queries, keys_here = pieces
        return masked_max(
            pair_scores(queries, own_rows),
            own_live[None, :] & (own_key[None, :] < keys_here[:, None]),
        )

    self_best = lax.map(self_max, (query_rows, query_key)).reshape(-1)
    first = side_bit == 0
    left_rows = jnp.where(first, own_rows, partner)
    left_key = jnp.where(first, own_key, partner_key)
    left_live = jnp.where(first, own_live, partner_live)
    right_rows = jnp.where(first, partner, own_rows)
    right_key = jnp.where(first, partner_key, own_key)
    right_live = jnp.where(first, partner_live, own_live)
    half_rows = buffer_rows // 2
    start = side_bit * half_rows
    lower_rows = lax.dynamic_slice_in_dim(left_rows, start, half_rows, 0).reshape(
        blocks // 2, -1, feature_dim
    )
    lower_key = lax.dynamic_slice_in_dim(left_key, start, half_rows, 0).reshape(blocks // 2, -1)
    lower_live = lax.dynamic_slice_in_dim(left_live, start, half_rows, 0).reshape(blocks // 2, -1)

    def cross_max(pieces):
        queries, keys_here, live_here = pieces
        scores = pair_scores(queries, right_rows)
        row_best = masked_max(
            scores, right_live[None, :] & (right_key[None, :] < keys_here[:, None])
        )
        column_mask = live_here[:, None] & (keys_here[:, None] < right_key[None, :])
        column_best = jnp.max(jnp.where(column_mask, scores, -1.0), axis=0)
        return (row_best, column_best)

    row_best, column_best = lax.map(cross_max, (lower_rows, lower_key, lower_live))
    row_best = row_best.reshape(-1)
    column_best = jnp.max(column_best, axis=0)
    placed = lax.dynamic_update_slice_in_dim(
        jnp.full((buffer_rows,), -1.0, jnp.float32), row_best, start, 0
    )
    kept = jnp.where(first, placed, column_best)
    handed = jnp.where(first, column_best, placed)
    returned = swapped(handed, "wide", 0)
    best_all = jnp.maximum(self_best, jnp.maximum(kept, returned))
    back = lax.all_to_all(
        best_all.reshape(axis_size, capacity), "wide", split_axis=0, concat_axis=0, tiled=True
    )
    return back.reshape(-1)[slot_index]


LANES = 4
PIECE = 64
CHUNK = 128
MESH = pl.DeviceIdType.MESH


def grid_kernel(levels, x_ref, id_ref, out_ref, lev, lev_id, unit, id_col, left, left_id, right,
                right_id, ferry, relay, acc, query_best, part, res, back, back_in,
                lev_send, lev_recv, left_send, left_recv, right_send, right_recv,
                ferry_send, ferry_recv, relay_send, relay_recv, hand_send,
                res_send, res_recv, back_send, back_recv):
    plane = lax.axis_index("dom")
    other = 1 - plane
    me = lax.axis_index("wide")
    lane = lax.rem(me, LANES)
    place = me // LANES
    base = place * LANES
    half = levels // 2
    rows, width = x_ref.shape
    count = rows // PIECE
    chunks = rows // CHUNK
    up = plane == 0
    level = jnp.where(up, place, levels - 1 - place)
    step = jnp.where(up, LANES, -LANES)
    relay_level = levels - 1 - level
    detour = [p for p in range(count) if p % 2 and p > 1]
    direct = [p for p in range(count) if p not in detour]

    def at_level(wanted):
        return me + (wanted - level) * step

    def peer(slot):
        low = lax.rem(lane, 2)
        high = lane // 2
        low = 1 - low if slot % 2 else low
        high = 1 - high if slot // 2 else high
        return base + 2 * high + low

    has_next = level < levels - 1
    sends_own = level < half
    takes_back = level == half
    gives_back = level == half + 1

    barrier = pltpu.get_barrier_semaphore()
    for slot in range(1, LANES):
        pl.semaphore_signal(barrier, inc=1, device_id={"dom": plane, "wide": peer(slot)},
                            device_id_type=MESH)
    for far in range(1, levels):
        there = lax.rem(place + far, levels) * LANES + lane
        pl.semaphore_signal(barrier, inc=1, device_id={"dom": plane, "wide": there},
                            device_id_type=MESH)
    pl.semaphore_signal(barrier, inc=1, device_id={"dom": other, "wide": me}, device_id_type=MESH)
    pl.semaphore_wait(barrier, LANES + levels - 1)

    def piece(block, ids, p):
        return ids if p == count else block.at[pl.ds(p * PIECE, PIECE)]

    order = [count] + list(range(count))

    def send(src, src_id, dst, dst_id, p, ssem, rsem, dev, row=None):
        return pltpu.make_async_remote_copy(
            src_ref=piece(src, src_id, p), dst_ref=piece(dst, dst_id, p),
            send_sem=ssem.at[p], recv_sem=rsem.at[p],
            device_id={"dom": plane if row is None else row, "wide": dev}, device_id_type=MESH)

    def level_own(slot, p):
        return send(x_ref, id_ref, lev.at[slot - 1], lev_id.at[slot - 1], p,
                    lev_send.at[slot - 1], lev_recv.at[slot - 1], peer(slot))

    def level_pass(p):
        return send(lev.at[1], lev_id.at[1], lev.at[2], lev_id.at[2], p,
                    lev_send.at[2], lev_recv.at[2], peer(1))

    def next_own(p):
        return send(x_ref, id_ref, left.at[0], left_id.at[0], p,
                    left_send.at[0], left_recv.at[0], me + step)

    def next_pass(j, to, p):
        return send(left.at[j], left_id.at[j], left.at[to], left_id.at[to], p,
                    left_send.at[to], left_recv.at[to], me + step)

    def back_own(p):
        return send(x_ref, id_ref, right, right_id, p, right_send, right_recv, me - step)

    def ferry_out(p):
        return send(x_ref, None, ferry, None, p, ferry_send, ferry_recv, me, other)

    def relay_own(p):
        return send(ferry, None, relay.at[0], None, p, relay_send.at[0], relay_recv.at[0],
                    me - step)

    def relay_pass(j, to, p):
        return send(relay.at[j], None, relay.at[to], None, p, relay_send.at[to],
                    relay_recv.at[to], me - step)

    def hand(j, p):
        return send(relay.at[j], None, left.at[j], None, p, hand_send.at[j], left_recv.at[j],
                    me, other)

    for p in order:
        @pl.when(sends_own)
        def _(p=p):
            (ferry_out if p in detour else next_own)(p).start()

        level_own(2, p).start()
        level_own(1, p).start()

        @pl.when(gives_back)
        def _(p=p):
            back_own(p).start()

    def normal(block):
        values = block.astype(jnp.float32)
        inverse = lax.rsqrt(jnp.mean(values * values, axis=1, keepdims=True) + 1e-06)
        return (values * inverse * (1.0 / math.sqrt(width))).astype(jnp.bfloat16)

    def column(ids, k):
        row = ids[:, k * CHUNK:(k + 1) * CHUNK]
        return jnp.transpose(jnp.broadcast_to(row, (CHUNK, CHUNK)))

    def scores(keys, queries):
        return lax.dot_general(keys, queries, (((1,), (1,)), ((), ())),
                               preferred_element_type=jnp.float32)

    def fold(values):
        tall, wide_by = values.shape
        return jnp.max(values.reshape(tall // 8, 8, wide_by), axis=0)

    def ids_of(slot):
        return id_ref if slot == 0 else lev_id.at[slot - 1]

    def unit_chunk(slot, k):
        at = pl.ds(k * CHUNK, CHUNK)
        unit[slot, at, :] = normal(x_ref[at, :] if slot == 0 else lev[slot - 1, at, :])
        id_col[slot, at, :] = column(ids_of(slot), k)

    def own_level(slot):
        best = acc[0]
        for k in range(chunks):
            at = pl.ds(k * CHUNK, CHUNK)
            value = scores(unit[slot, at, :], unit[0])
            keep = id_col[slot, at, :][:, :1] == id_ref[...]
            if slot == 0:
                key_at = lax.broadcasted_iota(jnp.int32, value.shape, 0) + k * CHUNK
                keep = keep & (key_at < lax.broadcasted_iota(jnp.int32, value.shape, 1))
            best = jnp.maximum(best, fold(jnp.where(keep, value, -1.0)))
        acc[0] = best

    def earlier_level(slot):
        @pl.when(peer(slot) < me)
        def _():
            own_level(slot)

    def as_keys(block, ids, k, slots):
        keys = normal(block[pl.ds(k * CHUNK, CHUNK), :])
        key_ids = column(ids, k)[:, :1]
        for slot in slots:
            value = scores(keys, unit[slot])
            value = jnp.where(key_ids == ids_of(slot)[...], value, -1.0)
            acc[slot] = jnp.maximum(acc[slot], fold(value))

    def as_queries(block, ids, best_at, k, slots):
        queries = normal(block[pl.ds(k * CHUNK, CHUNK), :])
        query_ids = ids[:, k * CHUNK:(k + 1) * CHUNK]
        best = query_best[best_at, :, k * CHUNK:(k + 1) * CHUNK]
        for slot in slots:
            value = scores(unit[slot], queries)
            value = jnp.where(id_col[slot] == query_ids, value, -1.0)
            best = jnp.maximum(best, fold(value))
        query_best[best_at, :, k * CHUNK:(k + 1) * CHUNK] = best

    def from_left(j, k, slots):
        @pl.when((level > j) & up)
        def _():
            as_keys(left.at[j], left_id.at[j], k, slots)

        @pl.when((level > j) & jnp.logical_not(up))
        def _():
            as_queries(left.at[j], left_id.at[j], j, k, slots)

    def from_right(k, slots):
        @pl.when(takes_back & up)
        def _():
            as_queries(right, right_id, half, k, slots)

        @pl.when(takes_back & jnp.logical_not(up))
        def _():
            as_keys(right, right_id, k, slots)

    def left_wait(j, p):
        (next_own(p) if j == 0 else next_pass(j - 1, j, p)).wait_recv()

    def left_step(j, p):
        @pl.when(level > j)
        def _():
            left_wait(j, p)
            if j + 1 < half:
                @pl.when(sends_own)
                def _():
                    next_pass(j, j + 1, p).start()

            @pl.when(has_next & jnp.logical_not(sends_own))
            def _():
                next_pass(j, j, p).start()

    def left_rest(j, k):
        for p in detour:
            if p * PIECE // CHUNK == k:
                @pl.when(level > j)
                def _(p=p):
                    left_wait(j, p)

    def ferry_step(p):
        @pl.when(relay_level < half)
        def _():
            ferry_out(p).wait_recv()
            relay_own(p).start()

    def relay_step(j, p):
        @pl.when(relay_level > j)
        def _():
            (relay_own(p) if j == 0 else relay_pass(j - 1, j, p)).wait_recv()
            if j + 1 < half:
                @pl.when(relay_level < half)
                def _():
                    relay_pass(j, j + 1, p).start()

            @pl.when((relay_level < levels - 1) & (relay_level >= half))
            def _():
                relay_pass(j, j, p).start()

            hand(j, p).start()

    def right_wait(k):
        for p in range(k * CHUNK // PIECE, (k + 1) * CHUNK // PIECE):
            @pl.when(takes_back)
            def _(p=p):
                back_own(p).wait_recv()

    acc[...] = jnp.full_like(acc, -1.0)
    query_best[...] = jnp.full_like(query_best, -1.0)
    for k in range(chunks):
        unit_chunk(0, k)

    near, far = (0, 1), (2, 3)
    level_own(2, count).wait_recv()
    level_pass(count).start()
    level_own(1, count).wait_recv()
    left_step(0, count)

    @pl.when(takes_back)
    def _():
        back_own(count).wait_recv()

    shift = len(direct)
    for t in range(count):
        if t < len(direct):
            left_step(0, direct[t])
        elif t - shift < len(direct):
            if t == shift:
                left_step(1, count)
            left_step(1, direct[t - shift])
        if t < len(detour):
            ferry_step(detour[t])
        if 0 <= t - 2 < len(detour):
            relay_step(0, detour[t - 2])
        if 0 <= t - shift < len(detour):
            relay_step(1, detour[t - shift])
        level_own(2, t).wait_recv()
        level_pass(t).start()
        if t == 0:
            own_level(0)
        if t == 2:
            for p in range(count):
                level_own(1, p).wait_recv()
            for k in range(chunks):
                unit_chunk(1, k)
        if t == 3:
            earlier_level(1)
        if t == 4:
            from_left(0, 0, near)
        if t == 5:
            right_wait(0)
            from_right(0, near)
        if t == 6:
            left_rest(0, 1)
            from_left(0, 1, near)
        if t == 7:
            right_wait(1)
            from_right(1, near)
        if t % 2:
            unit_chunk(2, t // 2)
    level_pass(count).wait_recv()
    for t in range(count, shift + len(direct)):
        left_step(1, direct[t - shift])
        k = t - count
        if k == 0:
            earlier_level(2)
        if k == 1:
            left_rest(0, 2)
            from_left(0, 2, near)
    for p in range(count):
        level_pass(p).wait_recv()
    for k in range(chunks):
        unit_chunk(3, k)
    earlier_level(3)
    left_rest(0, 3)
    from_left(0, 3, near)
    for k in range(chunks):
        from_left(0, k, far)
    for k in range(chunks):
        if k < 2:
            from_right(k, far)
        else:
            right_wait(k)
            from_right(k, near + far)
    for k in range(chunks):
        left_rest(1, k)
        from_left(1, k, near + far)

    def res_copy(slot):
        return pltpu.make_async_remote_copy(
            src_ref=part.at[slot - 1], dst_ref=res.at[slot - 1], send_sem=res_send.at[slot - 1],
            recv_sem=res_recv.at[slot - 1], device_id={"dom": plane, "wide": peer(slot)},
            device_id_type=MESH)

    def back_copy(which, source, wanted):
        return pltpu.make_async_remote_copy(
            src_ref=back.at[which], dst_ref=back_in.at[source - 1], send_sem=back_send.at[which],
            recv_sem=back_recv.at[source - 1], device_id={"dom": plane, "wide": at_level(wanted)},
            device_id_type=MESH)

    def backs(act):
        @pl.when(up & takes_back)
        def _():
            act(half, half, half + 1)

        for source in range(1, levels):
            for j in range(min(source, half)):
                @pl.when(jnp.logical_not(up) & (level == source))
                def _(source=source, j=j):
                    act(j, source, min(source, half) - 1 - j)

    def back_start(which, source, wanted):
        back[which] = jnp.max(query_best[which], axis=0, keepdims=True)
        back_copy(which, source, wanted).start()

    backs(back_start)
    for slot in (3, 2, 1):
        part[slot - 1] = jnp.max(acc[slot], axis=0, keepdims=True)
        res_copy(slot).start()
    out_ref[...] = jnp.max(acc[0], axis=0, keepdims=True)
    for slot in range(1, LANES):
        res_copy(slot).wait_recv()
        out_ref[...] = jnp.maximum(out_ref[...], res[slot - 1])

    def take(source):
        back_copy(0, source, 0).wait_recv()
        out_ref[...] = jnp.maximum(out_ref[...], back_in[source - 1])

    @pl.when(up & gives_back)
    def _():
        take(half)

    for source in range(1, levels):
        @pl.when(jnp.logical_not(up) & (level < min(source, half)))
        def _(source=source):
            take(source)

    backs(lambda which, source, wanted: back_copy(which, source, wanted).wait_send())
    for slot in range(1, LANES):
        res_copy(slot).wait_send()
    for p in order:
        level_own(2, p).wait_send()
        level_own(1, p).wait_send()
        level_pass(p).wait_send()

        @pl.when(sends_own)
        def _(p=p):
            (ferry_out if p in detour else next_own)(p).wait_send()

        @pl.when(gives_back)
        def _(p=p):
            back_own(p).wait_send()

        for j in range(half):
            if p in detour:
                @pl.when(relay_level > j)
                def _(j=j, p=p):
                    hand(j, p).wait_send()

                if j + 1 < half:
                    @pl.when((relay_level < half) & (relay_level > j))
                    def _(j=j, p=p):
                        relay_pass(j, j + 1, p).wait_send()

                @pl.when((relay_level < levels - 1) & (relay_level >= half))
                def _(j=j, p=p):
                    relay_pass(j, j, p).wait_send()
            else:
                if j + 1 < half:
                    @pl.when(sends_own & (level > j))
                    def _(j=j, p=p):
                        next_pass(j, j + 1, p).wait_send()

                @pl.when(has_next & jnp.logical_not(sends_own))
                def _(j=j, p=p):
                    next_pass(j, j, p).wait_send()
        if p in detour:
            @pl.when(relay_level < half)
            def _(p=p):
                relay_own(p).wait_send()


def grid_plan(levels, embeddings, cluster_id):
    rows, width = embeddings.shape
    half = levels // 2
    pieces = rows // PIECE + 1
    bf16, i32, f32 = jnp.bfloat16, jnp.int32, jnp.float32
    dma = pltpu.SemaphoreType.DMA
    vmem = pltpu.VMEM
    best = pl.pallas_call(
        functools.partial(grid_kernel, levels),
        out_shape=jax.ShapeDtypeStruct((1, rows), f32),
        in_specs=[pl.BlockSpec(memory_space=vmem)] * 2,
        out_specs=pl.BlockSpec(memory_space=vmem),
        scratch_shapes=[
            vmem((LANES - 1, rows, width), bf16), vmem((LANES - 1, 1, rows), i32),
            vmem((LANES, rows, width), bf16), vmem((LANES, rows, CHUNK), i32),
            vmem((half, rows, width), bf16), vmem((half, 1, rows), i32),
            vmem((rows, width), bf16), vmem((1, rows), i32),
            vmem((rows, width), bf16), vmem((half, rows, width), bf16),
            vmem((LANES, 8, rows), f32), vmem((half + 1, 8, rows), f32),
            vmem((LANES - 1, 1, rows), f32), vmem((LANES - 1, 1, rows), f32),
            vmem((half + 1, 1, rows), f32), vmem((levels - 1, 1, rows), f32),
            dma((LANES - 1, pieces)), dma((LANES - 1, pieces)),
            dma((half, pieces)), dma((half, pieces)),
            dma((pieces,)), dma((pieces,)),
            dma((pieces,)), dma((pieces,)),
            dma((half, pieces)), dma((half, pieces)), dma((half, pieces)),
            dma((LANES - 1,)), dma((LANES - 1,)),
            dma((half + 1,)), dma((levels - 1,)),
        ],
        compiler_params=pltpu.CompilerParams(
            collective_id=0, has_side_effects=True, vmem_limit_bytes=40 * 2**20),
    )(embeddings, cluster_id.reshape(1, rows))
    return best.reshape(-1)


def solution(mesh):
    placed = (P(("dom", "wide"), None), P(("dom", "wide"), None))
    levels = mesh.shape["wide"] // LANES
    fits = levels == 4 and mesh.shape["wide"] % LANES == 0 and mesh.shape["dom"] == 2
    plan = functools.partial(grid_plan, levels) if fits else per_device
    return jax.shard_map(
        plan, mesh=mesh, in_specs=placed, out_specs=P(("dom", "wide")), check_vma=False
    )
```

```python
import functools
import math

import jax
import jax.numpy as jnp
from jax import lax
from jax.experimental import pallas as pl
from jax.experimental.pallas import tpu as pltpu
from jax.sharding import PartitionSpec as P


def swapped(value, axis, bit):
    mask = 2**bit
    pairs = [(source, source ^ mask) for source in range(lax.axis_size(axis))]
    return lax.ppermute(value, axis, pairs)


def normalize(embedded):
    values = embedded.astype(jnp.float32)
    inverse = lax.rsqrt(jnp.mean(values * values, axis=1, keepdims=True) + 1e-06)
    return (values * inverse * (1.0 / math.sqrt(values.shape[1]))).astype(jnp.bfloat16)


def pair_scores(queries, key_rows):
    return jnp.einsum("qd,kd->qk", queries, key_rows, preferred_element_type=jnp.float32)


def masked_max(scores, allowed):
    return jnp.max(jnp.where(allowed, scores, -1.0), axis=1)


def per_device(embeddings, cluster_id):
    axis_size = lax.axis_size("wide")
    rows_dev = embeddings.shape[0]
    feature_dim = embeddings.shape[1]
    clusters = axis_size // 2
    capacity = (5 * rows_dev + 2 * axis_size - 1) // (2 * axis_size)
    buffer_rows = axis_size * capacity
    unit_rows = normalize(embeddings)
    labels = cluster_id[:, 0]
    my_index = lax.axis_index("wide")
    my_flip = my_index % 2
    position = lax.iota(jnp.int32, rows_dev)
    same_cluster = labels[:, None] == labels[None, :]
    earlier = position[None, :] < position[:, None]
    local_rank = jnp.sum((same_cluster & earlier).astype(jnp.int32), axis=1)
    target = 2 * labels + (local_rank + my_flip) % 2
    slot_index = target * capacity + local_rank // 2
    outgoing = jnp.zeros((buffer_rows, feature_dim), jnp.bfloat16).at[slot_index].set(unit_rows)
    cluster_count = jnp.sum(
        (labels[:, None] == lax.iota(jnp.int32, clusters)[None, :]).astype(jnp.int32), axis=0
    )
    parity = lax.iota(jnp.int32, axis_size) % 2
    send_count = (jnp.repeat(cluster_count, 2) + 1 - (parity + my_flip) % 2) // 2
    outgoing_blocks = outgoing.reshape(axis_size, capacity, feature_dim)
    count_blocks = send_count.reshape(axis_size, 1)
    received, counts = (
        lax.all_to_all(outgoing_blocks, "wide", split_axis=0, concat_axis=0, tiled=True),
        lax.all_to_all(count_blocks, "wide", split_axis=0, concat_axis=0, tiled=True),
    )
    own_rows = received.reshape(buffer_rows, feature_dim)
    partner, partner_counts = swapped((own_rows, counts), "wide", 0)
    side_bit = my_index % 2
    slot_pos = lax.iota(jnp.int32, capacity)
    sources = lax.iota(jnp.int32, axis_size)
    base_key = (sources[:, None] * (2 * capacity) + 2 * slot_pos[None, :]).reshape(-1)
    source_parity = jnp.repeat(sources % 2, capacity)
    own_key = base_key + (side_bit + source_parity) % 2
    partner_key = base_key + (1 - side_bit + source_parity) % 2
    own_live = (slot_pos[None, :] < counts).reshape(-1)
    partner_live = (slot_pos[None, :] < partner_counts).reshape(-1)
    blocks = 8
    query_rows = own_rows.reshape(blocks, -1, feature_dim)
    query_key = own_key.reshape(blocks, -1)

    def self_max(pieces):
        queries, keys_here = pieces
        return masked_max(
            pair_scores(queries, own_rows),
            own_live[None, :] & (own_key[None, :] < keys_here[:, None]),
        )

    self_best = lax.map(self_max, (query_rows, query_key)).reshape(-1)
    first = side_bit == 0
    left_rows = jnp.where(first, own_rows, partner)
    left_key = jnp.where(first, own_key, partner_key)
    left_live = jnp.where(first, own_live, partner_live)
    right_rows = jnp.where(first, partner, own_rows)
    right_key = jnp.where(first, partner_key, own_key)
    right_live = jnp.where(first, partner_live, own_live)
    half_rows = buffer_rows // 2
    start = side_bit * half_rows
    lower_rows = lax.dynamic_slice_in_dim(left_rows, start, half_rows, 0).reshape(
        blocks // 2, -1, feature_dim
    )
    lower_key = lax.dynamic_slice_in_dim(left_key, start, half_rows, 0).reshape(blocks // 2, -1)
    lower_live = lax.dynamic_slice_in_dim(left_live, start, half_rows, 0).reshape(blocks // 2, -1)

    def cross_max(pieces):
        queries, keys_here, live_here = pieces
        scores = pair_scores(queries, right_rows)
        row_best = masked_max(
            scores, right_live[None, :] & (right_key[None, :] < keys_here[:, None])
        )
        column_mask = live_here[:, None] & (keys_here[:, None] < right_key[None, :])
        column_best = jnp.max(jnp.where(column_mask, scores, -1.0), axis=0)
        return (row_best, column_best)

    row_best, column_best = lax.map(cross_max, (lower_rows, lower_key, lower_live))
    row_best = row_best.reshape(-1)
    column_best = jnp.max(column_best, axis=0)
    placed = lax.dynamic_update_slice_in_dim(
        jnp.full((buffer_rows,), -1.0, jnp.float32), row_best, start, 0
    )
    kept = jnp.where(first, placed, column_best)
    handed = jnp.where(first, column_best, placed)
    returned = swapped(handed, "wide", 0)
    best_all = jnp.maximum(self_best, jnp.maximum(kept, returned))
    back = lax.all_to_all(
        best_all.reshape(axis_size, capacity), "wide", split_axis=0, concat_axis=0, tiled=True
    )
    return back.reshape(-1)[slot_index]


LANES = 4
PIECE = 64
CHUNK = 128
MESH = pl.DeviceIdType.MESH


def grid_kernel(levels, x_ref, id_ref, out_ref, lev, lev_id, unit, id_col, left, left_id, right,
                right_id, acc, query_best, part, res, back, back_in,
                lev_send, lev_recv, left_send, left_recv, right_send, right_recv,
                res_send, res_recv, back_send, back_recv):
    me = lax.axis_index("wide")
    lane = lax.rem(me, LANES)
    level = me // LANES
    base = level * LANES
    half = levels // 2
    rows, width = x_ref.shape
    count = rows // PIECE
    chunks = rows // CHUNK
    def peer(slot):
        low = lax.rem(lane, 2)
        high = lane // 2
        low = 1 - low if slot % 2 else low
        high = 1 - high if slot // 2 else high
        return base + 2 * high + low

    has_next = level < levels - 1
    sends_own = level < half
    takes_back = level == half
    gives_back = level == half + 1

    barrier = pltpu.get_barrier_semaphore()
    for slot in range(1, LANES):
        pl.semaphore_signal(barrier, inc=1, device_id={"wide": peer(slot)}, device_id_type=MESH)

    @pl.when(has_next)
    def _():
        pl.semaphore_signal(barrier, inc=1, device_id={"wide": me + LANES}, device_id_type=MESH)

    @pl.when(level > 0)
    def _():
        pl.semaphore_signal(barrier, inc=1, device_id={"wide": me - LANES}, device_id_type=MESH)

    peers = LANES - 1 + has_next.astype(jnp.int32) + (level > 0).astype(jnp.int32)
    pl.semaphore_wait(barrier, peers)

    def piece(block, ids, p):
        return ids if p == count else block.at[pl.ds(p * PIECE, PIECE)]

    order = [count] + list(range(count))

    def send(src, src_id, dst, dst_id, p, ssem, rsem, dev):
        return pltpu.make_async_remote_copy(
            src_ref=piece(src, src_id, p), dst_ref=piece(dst, dst_id, p),
            send_sem=ssem.at[p], recv_sem=rsem.at[p],
            device_id={"wide": dev}, device_id_type=MESH)

    def level_own(slot, p):
        return send(x_ref, id_ref, lev.at[slot - 1], lev_id.at[slot - 1], p,
                    lev_send.at[slot - 1], lev_recv.at[slot - 1], peer(slot))

    def level_pass(p):
        return send(lev.at[1], lev_id.at[1], lev.at[2], lev_id.at[2], p,
                    lev_send.at[2], lev_recv.at[2], peer(1))

    def next_own(p):
        return send(x_ref, id_ref, left.at[0], left_id.at[0], p,
                    left_send.at[0], left_recv.at[0], me + LANES)

    def next_pass(j, to, p):
        return send(left.at[j], left_id.at[j], left.at[to], left_id.at[to], p,
                    left_send.at[to], left_recv.at[to], me + LANES)

    def back_own(p):
        return send(x_ref, id_ref, right, right_id, p, right_send, right_recv, me - LANES)

    for p in order:
        @pl.when(sends_own)
        def _(p=p):
            next_own(p).start()

        level_own(2, p).start()
        level_own(1, p).start()

        @pl.when(gives_back)
        def _(p=p):
            back_own(p).start()

    def normal(block):
        values = block.astype(jnp.float32)
        inverse = lax.rsqrt(jnp.mean(values * values, axis=1, keepdims=True) + 1e-06)
        return (values * inverse * (1.0 / math.sqrt(width))).astype(jnp.bfloat16)

    def column(ids, k):
        row = ids[:, k * CHUNK:(k + 1) * CHUNK]
        return jnp.transpose(jnp.broadcast_to(row, (CHUNK, CHUNK)))

    def scores(keys, queries):
        return lax.dot_general(keys, queries, (((1,), (1,)), ((), ())),
                               preferred_element_type=jnp.float32)

    def fold(values):
        tall, wide_by = values.shape
        return jnp.max(values.reshape(tall // 8, 8, wide_by), axis=0)

    def ids_of(slot):
        return id_ref if slot == 0 else lev_id.at[slot - 1]

    def unit_chunk(slot, k):
        at = pl.ds(k * CHUNK, CHUNK)
        unit[slot, at, :] = normal(x_ref[at, :] if slot == 0 else lev[slot - 1, at, :])
        id_col[slot, at, :] = column(ids_of(slot), k)

    def own_level(slot):
        best = acc[0]
        for k in range(chunks):
            at = pl.ds(k * CHUNK, CHUNK)
            value = scores(unit[slot, at, :], unit[0])
            keep = id_col[slot, at, :][:, :1] == id_ref[...]
            if slot == 0:
                key_at = lax.broadcasted_iota(jnp.int32, value.shape, 0) + k * CHUNK
                keep = keep & (key_at < lax.broadcasted_iota(jnp.int32, value.shape, 1))
            best = jnp.maximum(best, fold(jnp.where(keep, value, -1.0)))
        acc[0] = best

    def earlier_level(slot):
        @pl.when(peer(slot) < me)
        def _():
            own_level(slot)

    def as_keys(block, ids, k, slots):
        keys = normal(block[pl.ds(k * CHUNK, CHUNK), :])
        key_ids = column(ids, k)[:, :1]
        for slot in slots:
            value = scores(keys, unit[slot])
            value = jnp.where(key_ids == ids_of(slot)[...], value, -1.0)
            acc[slot] = jnp.maximum(acc[slot], fold(value))

    def as_queries(block, ids, k, slots):
        queries = normal(block[pl.ds(k * CHUNK, CHUNK), :])
        query_ids = ids[:, k * CHUNK:(k + 1) * CHUNK]
        best = query_best[:, k * CHUNK:(k + 1) * CHUNK]
        for slot in slots:
            value = scores(unit[slot], queries)
            value = jnp.where(id_col[slot] == query_ids, value, -1.0)
            best = jnp.maximum(best, fold(value))
        query_best[:, k * CHUNK:(k + 1) * CHUNK] = best

    def from_left(j, k, slots):
        @pl.when(level > j)
        def _():
            as_keys(left.at[j], left_id.at[j], k, slots)

    def from_right(k, slots):
        @pl.when(takes_back)
        def _():
            as_queries(right, right_id, k, slots)

    def left_wait(j, p):
        (next_own(p) if j == 0 else next_pass(j - 1, j, p)).wait_recv()

    def left_step(j, p):
        @pl.when(level > j)
        def _():
            left_wait(j, p)
            if j + 1 < half:
                @pl.when(sends_own)
                def _():
                    next_pass(j, j + 1, p).start()

            @pl.when(has_next & jnp.logical_not(sends_own))
            def _():
                next_pass(j, j, p).start()

    def right_wait(k):
        for p in range(k * CHUNK // PIECE, (k + 1) * CHUNK // PIECE):
            @pl.when(takes_back)
            def _(p=p):
                back_own(p).wait_recv()

    acc[...] = jnp.full_like(acc, -1.0)
    query_best[...] = jnp.full_like(query_best, -1.0)
    for k in range(chunks):
        unit_chunk(0, k)

    def res_copy(slot):
        return pltpu.make_async_remote_copy(
            src_ref=part.at[slot - 1], dst_ref=res.at[slot - 1], send_sem=res_send.at[slot - 1],
            recv_sem=res_recv.at[slot - 1], device_id={"wide": peer(slot)}, device_id_type=MESH)

    def back_copy():
        return pltpu.make_async_remote_copy(
            src_ref=back, dst_ref=back_in, send_sem=back_send, recv_sem=back_recv,
            device_id={"wide": me + LANES}, device_id_type=MESH)

    near, far = (0, 1), (2, 3)
    level_own(2, count).wait_recv()
    level_pass(count).start()
    level_own(1, count).wait_recv()
    left_step(0, count)

    @pl.when(takes_back)
    def _():
        back_own(count).wait_recv()

    for t in range(count):
        left_step(0, t)
        level_own(2, t).wait_recv()
        level_pass(t).start()
        if t == 0:
            own_level(0)
        if t == 2:
            for p in range(count):
                level_own(1, p).wait_recv()
            for k in range(chunks):
                unit_chunk(1, k)
        if t == 3:
            earlier_level(1)
            from_left(0, 0, near)
        if t == 4:
            right_wait(0)
            from_right(0, near)
        if t == 5:
            from_left(0, 1, near)
            right_wait(1)
            from_right(1, near)
        if t == 6:
            from_left(0, 2, near)
        if t % 2:
            unit_chunk(2, t // 2)
    level_pass(count).wait_recv()
    for p in range(count):
        level_pass(p).wait_recv()
    left_step(1, count)
    for t in range(count):
        left_step(1, t)
        k = t // 2
        if t == 0:
            from_left(0, 3, near)
            for at in range(chunks):
                unit_chunk(3, at)
        if t == 1:
            earlier_level(2)
            earlier_level(3)
        if t == 2:
            from_left(0, 0, far)
            from_left(1, 0, near + far)
        if t == 3:
            from_left(0, 1, far)
            from_right(0, far)
        if t == 4:
            from_left(0, 2, far)
            from_right(1, far)
        if t == 5:
            from_left(0, 3, far)
            from_left(1, 1, near + far)
        if t == 6:
            right_wait(2)
            from_right(2, near + far)
            from_left(1, 2, near + far)
        if t == 7:
            right_wait(3)
            from_right(3, near + far)

            @pl.when(takes_back)
            def _():
                back[...] = jnp.max(query_best[...], axis=0, keepdims=True)
                back_copy().start()

            from_left(1, 3, near + far)

    for slot in (3, 2, 1):
        part[slot - 1] = jnp.max(acc[slot], axis=0, keepdims=True)
        res_copy(slot).start()
    out_ref[...] = jnp.max(acc[0], axis=0, keepdims=True)
    for slot in range(1, LANES):
        res_copy(slot).wait_recv()
        out_ref[...] = jnp.maximum(out_ref[...], res[slot - 1])

    @pl.when(gives_back)
    def _():
        back_copy().wait_recv()
        out_ref[...] = jnp.maximum(out_ref[...], back_in[...])

    @pl.when(takes_back)
    def _():
        back_copy().wait_send()

    for slot in range(1, LANES):
        res_copy(slot).wait_send()
    for p in order:
        level_own(2, p).wait_send()
        level_own(1, p).wait_send()
        level_pass(p).wait_send()

        @pl.when(sends_own)
        def _(p=p):
            next_own(p).wait_send()

        @pl.when(gives_back)
        def _(p=p):
            back_own(p).wait_send()

        for j in range(half):
            if j + 1 < half:
                @pl.when(sends_own & (level > j))
                def _(j=j, p=p):
                    next_pass(j, j + 1, p).wait_send()

            @pl.when(has_next & jnp.logical_not(sends_own))
            def _(j=j, p=p):
                next_pass(j, j, p).wait_send()


def grid_plan(levels, embeddings, cluster_id):
    rows, width = embeddings.shape
    half = levels // 2
    pieces = rows // PIECE + 1
    bf16, i32, f32 = jnp.bfloat16, jnp.int32, jnp.float32
    dma = pltpu.SemaphoreType.DMA
    vmem = pltpu.VMEM
    best = pl.pallas_call(
        functools.partial(grid_kernel, levels),
        out_shape=jax.ShapeDtypeStruct((1, rows), f32),
        in_specs=[pl.BlockSpec(memory_space=vmem)] * 2,
        out_specs=pl.BlockSpec(memory_space=vmem),
        scratch_shapes=[
            vmem((LANES - 1, rows, width), bf16), vmem((LANES - 1, 1, rows), i32),
            vmem((LANES, rows, width), bf16), vmem((LANES, rows, CHUNK), i32),
            vmem((half, rows, width), bf16), vmem((half, 1, rows), i32),
            vmem((rows, width), bf16), vmem((1, rows), i32),
            vmem((LANES, 8, rows), f32), vmem((8, rows), f32),
            vmem((LANES - 1, 1, rows), f32), vmem((LANES - 1, 1, rows), f32),
            vmem((1, rows), f32), vmem((1, rows), f32),
            dma((LANES - 1, pieces)), dma((LANES - 1, pieces)),
            dma((half, pieces)), dma((half, pieces)),
            dma((pieces,)), dma((pieces,)),
            dma((LANES - 1,)), dma((LANES - 1,)),
            dma, dma,
        ],
        compiler_params=pltpu.CompilerParams(
            collective_id=0, has_side_effects=True, vmem_limit_bytes=40 * 2**20),
    )(embeddings, cluster_id.reshape(1, rows))
    return best.reshape(-1)


def solution(mesh):
    placed = (P(("dom", "wide"), None), P(("dom", "wide"), None))
    levels = mesh.shape["wide"] // LANES
    fits = levels == 4 and mesh.shape["wide"] % LANES == 0
    plan = functools.partial(grid_plan, levels) if fits else per_device
    return jax.shard_map(
        plan, mesh=mesh, in_specs=placed, out_specs=P(("dom", "wide")), check_vma=False
    )
```

```python
import functools
import math

import jax
import jax.numpy as jnp
from jax import lax
from jax.experimental import pallas as pl
from jax.experimental.pallas import tpu as pltpu
from jax.sharding import PartitionSpec as P


def swapped(value, axis, bit):
    mask = 2**bit
    pairs = [(source, source ^ mask) for source in range(lax.axis_size(axis))]
    return lax.ppermute(value, axis, pairs)


def normalize(embedded):
    values = embedded.astype(jnp.float32)
    inverse = lax.rsqrt(jnp.mean(values * values, axis=1, keepdims=True) + 1e-06)
    return (values * inverse * (1.0 / math.sqrt(values.shape[1]))).astype(jnp.bfloat16)


def pair_scores(queries, key_rows):
    return jnp.einsum("qd,kd->qk", queries, key_rows, preferred_element_type=jnp.float32)


def masked_max(scores, allowed):
    return jnp.max(jnp.where(allowed, scores, -1.0), axis=1)


def per_device(embeddings, cluster_id):
    axis_size = lax.axis_size("wide")
    rows_dev = embeddings.shape[0]
    feature_dim = embeddings.shape[1]
    clusters = axis_size // 2
    capacity = (5 * rows_dev + 2 * axis_size - 1) // (2 * axis_size)
    buffer_rows = axis_size * capacity
    unit_rows = normalize(embeddings)
    labels = cluster_id[:, 0]
    my_index = lax.axis_index("wide")
    my_flip = my_index % 2
    position = lax.iota(jnp.int32, rows_dev)
    same_cluster = labels[:, None] == labels[None, :]
    earlier = position[None, :] < position[:, None]
    local_rank = jnp.sum((same_cluster & earlier).astype(jnp.int32), axis=1)
    target = 2 * labels + (local_rank + my_flip) % 2
    slot_index = target * capacity + local_rank // 2
    outgoing = jnp.zeros((buffer_rows, feature_dim), jnp.bfloat16).at[slot_index].set(unit_rows)
    cluster_count = jnp.sum(
        (labels[:, None] == lax.iota(jnp.int32, clusters)[None, :]).astype(jnp.int32), axis=0
    )
    parity = lax.iota(jnp.int32, axis_size) % 2
    send_count = (jnp.repeat(cluster_count, 2) + 1 - (parity + my_flip) % 2) // 2
    outgoing_blocks = outgoing.reshape(axis_size, capacity, feature_dim)
    count_blocks = send_count.reshape(axis_size, 1)
    received, counts = (
        lax.all_to_all(outgoing_blocks, "wide", split_axis=0, concat_axis=0, tiled=True),
        lax.all_to_all(count_blocks, "wide", split_axis=0, concat_axis=0, tiled=True),
    )
    own_rows = received.reshape(buffer_rows, feature_dim)
    partner, partner_counts = swapped((own_rows, counts), "wide", 0)
    side_bit = my_index % 2
    slot_pos = lax.iota(jnp.int32, capacity)
    sources = lax.iota(jnp.int32, axis_size)
    base_key = (sources[:, None] * (2 * capacity) + 2 * slot_pos[None, :]).reshape(-1)
    source_parity = jnp.repeat(sources % 2, capacity)
    own_key = base_key + (side_bit + source_parity) % 2
    partner_key = base_key + (1 - side_bit + source_parity) % 2
    own_live = (slot_pos[None, :] < counts).reshape(-1)
    partner_live = (slot_pos[None, :] < partner_counts).reshape(-1)
    blocks = 8
    query_rows = own_rows.reshape(blocks, -1, feature_dim)
    query_key = own_key.reshape(blocks, -1)

    def self_max(pieces):
        queries, keys_here = pieces
        return masked_max(
            pair_scores(queries, own_rows),
            own_live[None, :] & (own_key[None, :] < keys_here[:, None]),
        )

    self_best = lax.map(self_max, (query_rows, query_key)).reshape(-1)
    first = side_bit == 0
    left_rows = jnp.where(first, own_rows, partner)
    left_key = jnp.where(first, own_key, partner_key)
    left_live = jnp.where(first, own_live, partner_live)
    right_rows = jnp.where(first, partner, own_rows)
    right_key = jnp.where(first, partner_key, own_key)
    right_live = jnp.where(first, partner_live, own_live)
    half_rows = buffer_rows // 2
    start = side_bit * half_rows
    lower_rows = lax.dynamic_slice_in_dim(left_rows, start, half_rows, 0).reshape(
        blocks // 2, -1, feature_dim
    )
    lower_key = lax.dynamic_slice_in_dim(left_key, start, half_rows, 0).reshape(blocks // 2, -1)
    lower_live = lax.dynamic_slice_in_dim(left_live, start, half_rows, 0).reshape(blocks // 2, -1)

    def cross_max(pieces):
        queries, keys_here, live_here = pieces
        scores = pair_scores(queries, right_rows)
        row_best = masked_max(
            scores, right_live[None, :] & (right_key[None, :] < keys_here[:, None])
        )
        column_mask = live_here[:, None] & (keys_here[:, None] < right_key[None, :])
        column_best = jnp.max(jnp.where(column_mask, scores, -1.0), axis=0)
        return (row_best, column_best)

    row_best, column_best = lax.map(cross_max, (lower_rows, lower_key, lower_live))
    row_best = row_best.reshape(-1)
    column_best = jnp.max(column_best, axis=0)
    placed = lax.dynamic_update_slice_in_dim(
        jnp.full((buffer_rows,), -1.0, jnp.float32), row_best, start, 0
    )
    kept = jnp.where(first, placed, column_best)
    handed = jnp.where(first, column_best, placed)
    returned = swapped(handed, "wide", 0)
    best_all = jnp.maximum(self_best, jnp.maximum(kept, returned))
    back = lax.all_to_all(
        best_all.reshape(axis_size, capacity), "wide", split_axis=0, concat_axis=0, tiled=True
    )
    return back.reshape(-1)[slot_index]


LANES = 4
PIECE = 64
CHUNK = 128
MESH = pl.DeviceIdType.MESH


def grid_kernel(levels, x_ref, id_ref, out_ref, own, own_sem, lev, lev_id, unit, id_col, left, left_id, right,
                right_id, acc, query_best, part, res, back, back_in,
                lev_send, lev_recv, left_send, left_recv, right_send, right_recv,
                res_send, res_recv, back_send, back_recv):
    me = lax.axis_index("wide")
    lane = lax.rem(me, LANES)
    level = me // LANES
    base = level * LANES
    half = levels // 2
    rows, width = x_ref.shape
    count = rows // PIECE
    chunks = rows // CHUNK
    def peer(slot):
        low = lax.rem(lane, 2)
        high = lane // 2
        low = 1 - low if slot % 2 else low
        high = 1 - high if slot // 2 else high
        return base + 2 * high + low

    has_next = level < levels - 1
    sends_own = level < half
    takes_back = level == half
    gives_back = level == half + 1

    own_copy = pltpu.make_async_copy(x_ref, own, own_sem)
    own_copy.start()
    barrier = pltpu.get_barrier_semaphore()
    for slot in range(1, LANES):
        pl.semaphore_signal(barrier, inc=1, device_id={"wide": peer(slot)}, device_id_type=MESH)

    @pl.when(has_next)
    def _():
        pl.semaphore_signal(barrier, inc=1, device_id={"wide": me + LANES}, device_id_type=MESH)

    @pl.when(level > 0)
    def _():
        pl.semaphore_signal(barrier, inc=1, device_id={"wide": me - LANES}, device_id_type=MESH)

    peers = LANES - 1 + has_next.astype(jnp.int32) + (level > 0).astype(jnp.int32)
    pl.semaphore_wait(barrier, peers)

    def piece(block, ids, p):
        return ids if p == count else block.at[pl.ds(p * PIECE, PIECE)]

    order = [count] + list(range(count))

    def send(src, src_id, dst, dst_id, p, ssem, rsem, dev):
        return pltpu.make_async_remote_copy(
            src_ref=piece(src, src_id, p), dst_ref=piece(dst, dst_id, p),
            send_sem=ssem.at[p], recv_sem=rsem.at[p],
            device_id={"wide": dev}, device_id_type=MESH)

    def level_own(slot, p):
        return send(x_ref, id_ref, lev.at[slot - 1], lev_id.at[slot - 1], p,
                    lev_send.at[slot - 1], lev_recv.at[slot - 1], peer(slot))

    def level_pass(p):
        return send(lev.at[1], lev_id.at[1], lev.at[2], lev_id.at[2], p,
                    lev_send.at[2], lev_recv.at[2], peer(1))

    def next_own(p):
        return send(x_ref, id_ref, left.at[0], left_id.at[0], p,
                    left_send.at[0], left_recv.at[0], me + LANES)

    def next_pass(j, to, p):
        return send(left.at[j], left_id.at[j], left.at[to], left_id.at[to], p,
                    left_send.at[to], left_recv.at[to], me + LANES)

    def back_own(p):
        return send(x_ref, id_ref, right, right_id, p, right_send, right_recv, me - LANES)

    for p in order:
        @pl.when(sends_own)
        def _(p=p):
            next_own(p).start()

        level_own(2, p).start()
        level_own(1, p).start()

        @pl.when(gives_back)
        def _(p=p):
            back_own(p).start()

    def normal(block):
        values = block.astype(jnp.float32)
        inverse = lax.rsqrt(jnp.mean(values * values, axis=1, keepdims=True) + 1e-06)
        return (values * inverse * (1.0 / math.sqrt(width))).astype(jnp.bfloat16)

    def column(ids, k):
        row = ids[:, k * CHUNK:(k + 1) * CHUNK]
        return jnp.transpose(jnp.broadcast_to(row, (CHUNK, CHUNK)))

    def scores(keys, queries):
        return lax.dot_general(keys, queries, (((1,), (1,)), ((), ())),
                               preferred_element_type=jnp.float32)

    def fold(values):
        tall, wide_by = values.shape
        return jnp.max(values.reshape(tall // 8, 8, wide_by), axis=0)

    def ids_of(slot):
        return id_ref if slot == 0 else lev_id.at[slot - 1]

    def unit_chunk(slot, k):
        at = pl.ds(k * CHUNK, CHUNK)
        unit[slot, at, :] = normal(own[at, :] if slot == 0 else lev[slot - 1, at, :])
        id_col[slot, at, :] = column(ids_of(slot), k)

    def own_level(slot):
        best = acc[0]
        for k in range(chunks):
            at = pl.ds(k * CHUNK, CHUNK)
            value = scores(unit[slot, at, :], unit[0])
            keep = id_col[slot, at, :][:, :1] == id_ref[...]
            if slot == 0:
                key_at = lax.broadcasted_iota(jnp.int32, value.shape, 0) + k * CHUNK
                keep = keep & (key_at < lax.broadcasted_iota(jnp.int32, value.shape, 1))
            best = jnp.maximum(best, fold(jnp.where(keep, value, -1.0)))
        acc[0] = best

    def earlier_level(slot):
        @pl.when(peer(slot) < me)
        def _():
            own_level(slot)

    def as_keys(block, ids, k, slots, begin=0, size=CHUNK):
        keys = normal(block[pl.ds(k * CHUNK + begin, size), :])
        key_ids = column(ids, k)[begin:begin + size, :1]
        for slot in slots:
            value = scores(keys, unit[slot])
            value = jnp.where(key_ids == ids_of(slot)[...], value, -1.0)
            acc[slot] = jnp.maximum(acc[slot], fold(value))

    def as_queries(block, ids, k, slots):
        queries = normal(block[pl.ds(k * CHUNK, CHUNK), :])
        query_ids = ids[:, k * CHUNK:(k + 1) * CHUNK]
        best = query_best[:, k * CHUNK:(k + 1) * CHUNK]
        for slot in slots:
            value = scores(unit[slot], queries)
            value = jnp.where(id_col[slot] == query_ids, value, -1.0)
            best = jnp.maximum(best, fold(value))
        query_best[:, k * CHUNK:(k + 1) * CHUNK] = best

    def from_left(j, k, slots, begin=0, size=CHUNK):
        @pl.when(level > j)
        def _():
            as_keys(left.at[j], left_id.at[j], k, slots, begin, size)

    def from_right(k, slots):
        @pl.when(takes_back)
        def _():
            as_queries(right, right_id, k, slots)

    def left_wait(j, p):
        (next_own(p) if j == 0 else next_pass(j - 1, j, p)).wait_recv()

    def left_step(j, p):
        @pl.when(level > j)
        def _():
            left_wait(j, p)
            if j + 1 < half:
                @pl.when(sends_own)
                def _():
                    next_pass(j, j + 1, p).start()

            @pl.when(has_next & jnp.logical_not(sends_own))
            def _():
                next_pass(j, j, p).start()

    def right_wait(k):
        for p in range(k * CHUNK // PIECE, (k + 1) * CHUNK // PIECE):
            @pl.when(takes_back)
            def _(p=p):
                back_own(p).wait_recv()

    own_copy.wait()
    acc[...] = jnp.full_like(acc, -1.0)
    query_best[...] = jnp.full_like(query_best, -1.0)
    for k in range(chunks):
        unit_chunk(0, k)

    def res_copy(slot):
        return pltpu.make_async_remote_copy(
            src_ref=part.at[slot - 1], dst_ref=res.at[slot - 1], send_sem=res_send.at[slot - 1],
            recv_sem=res_recv.at[slot - 1], device_id={"wide": peer(slot)}, device_id_type=MESH)

    def back_copy():
        return pltpu.make_async_remote_copy(
            src_ref=back, dst_ref=back_in, send_sem=back_send, recv_sem=back_recv,
            device_id={"wide": me + LANES}, device_id_type=MESH)

    near, far = (0, 1), (2, 3)
    level_own(2, count).wait_recv()
    level_pass(count).start()
    level_own(1, count).wait_recv()
    left_step(0, count)

    @pl.when(takes_back)
    def _():
        back_own(count).wait_recv()

    for t in range(count):
        left_step(0, t)
        level_own(2, t).wait_recv()
        level_pass(t).start()
        if t == 0:
            own_level(0)
        if t == 2:
            for p in range(count):
                level_own(1, p).wait_recv()
            for k in range(chunks):
                unit_chunk(1, k)
        if t == 3:
            earlier_level(1)
            from_left(0, 0, near)
        if t == 4:
            right_wait(0)
            from_right(0, near)
        if t == 5:
            from_left(0, 1, near)
            right_wait(1)
            from_right(1, near)
        if t == 6:
            from_left(0, 2, near)
        if t % 2:
            unit_chunk(2, t // 2)
    level_pass(count).wait_recv()
    for p in range(count):
        level_pass(p).wait_recv()
    left_step(1, count)
    for t in range(count):
        left_step(1, t)
        k = t // 2
        if t == 0:
            from_left(0, 3, near)
            for at in range(chunks):
                unit_chunk(3, at)
        if t == 1:
            earlier_level(2)
            earlier_level(3)
        if t == 2:
            from_left(0, 0, far)
            from_left(1, 0, near + far)
        if t == 3:
            from_left(0, 1, far)
            from_right(0, far)
        if t == 4:
            from_left(0, 2, far)
            from_right(1, far)
        if t == 5:
            from_left(0, 3, far)
            from_left(1, 1, near + far)
        if t == 6:
            right_wait(2)
            from_right(2, near + far)
            right_wait(3)
            from_right(3, near + far)
            from_left(1, 2, near + far)
            from_left(1, 3, near + far, 0, PIECE)
        if t == 7:

            @pl.when(takes_back)
            def _():
                back[...] = jnp.max(query_best[...], axis=0, keepdims=True)
                back_copy().start()

            from_left(1, 3, near + far, PIECE, PIECE)

    for slot in (3, 2, 1):
        part[slot - 1] = jnp.max(acc[slot], axis=0, keepdims=True)
        res_copy(slot).start()
    out_ref[...] = jnp.max(acc[0], axis=0, keepdims=True)
    for slot in range(1, LANES):
        res_copy(slot).wait_recv()
        out_ref[...] = jnp.maximum(out_ref[...], res[slot - 1])

    @pl.when(gives_back)
    def _():
        back_copy().wait_recv()
        out_ref[...] = jnp.maximum(out_ref[...], back_in[...])

    @pl.when(takes_back)
    def _():
        back_copy().wait_send()

    for slot in range(1, LANES):
        res_copy(slot).wait_send()
    for p in order:
        level_own(2, p).wait_send()
        level_own(1, p).wait_send()
        level_pass(p).wait_send()

        @pl.when(sends_own)
        def _(p=p):
            next_own(p).wait_send()

        @pl.when(gives_back)
        def _(p=p):
            back_own(p).wait_send()

        for j in range(half):
            if j + 1 < half:
                @pl.when(sends_own & (level > j))
                def _(j=j, p=p):
                    next_pass(j, j + 1, p).wait_send()

            @pl.when(has_next & jnp.logical_not(sends_own))
            def _(j=j, p=p):
                next_pass(j, j, p).wait_send()


def grid_plan(levels, embeddings, cluster_id):
    rows, width = embeddings.shape
    half = levels // 2
    pieces = rows // PIECE + 1
    bf16, i32, f32 = jnp.bfloat16, jnp.int32, jnp.float32
    dma = pltpu.SemaphoreType.DMA
    vmem = pltpu.VMEM
    best = pl.pallas_call(
        functools.partial(grid_kernel, levels),
        out_shape=jax.ShapeDtypeStruct((1, rows), f32),
        in_specs=[pl.BlockSpec(memory_space=pl.ANY), pl.BlockSpec(memory_space=vmem)],
        out_specs=pl.BlockSpec(memory_space=vmem),
        scratch_shapes=[
            vmem((rows, width), bf16), dma,
            vmem((LANES - 1, rows, width), bf16), vmem((LANES - 1, 1, rows), i32),
            vmem((LANES, rows, width), bf16), vmem((LANES, rows, CHUNK), i32),
            vmem((half, rows, width), bf16), vmem((half, 1, rows), i32),
            vmem((rows, width), bf16), vmem((1, rows), i32),
            vmem((LANES, 8, rows), f32), vmem((8, rows), f32),
            vmem((LANES - 1, 1, rows), f32), vmem((LANES - 1, 1, rows), f32),
            vmem((1, rows), f32), vmem((1, rows), f32),
            dma((LANES - 1, pieces)), dma((LANES - 1, pieces)),
            dma((half, pieces)), dma((half, pieces)),
            dma((pieces,)), dma((pieces,)),
            dma((LANES - 1,)), dma((LANES - 1,)),
            dma, dma,
        ],
        compiler_params=pltpu.CompilerParams(
            collective_id=0, has_side_effects=True, vmem_limit_bytes=40 * 2**20),
    )(embeddings, cluster_id.reshape(1, rows))
    return best.reshape(-1)


def solution(mesh):
    placed = (P(("dom", "wide"), None), P(("dom", "wide"), None))
    levels = mesh.shape["wide"] // LANES
    fits = levels == 4 and mesh.shape["wide"] % LANES == 0
    plan = functools.partial(grid_plan, levels) if fits else per_device
    return jax.shard_map(
        plan, mesh=mesh, in_specs=placed, out_specs=P(("dom", "wide")), check_vma=False
    )
```
